256 devices in a mesh: section: 8 (over z), neuron: 32 (over y, x, core).
Axes of the slice: x: 4, y: 4, z: 8, core: 2. Of those that a mesh axis runs over, the one named last changes fastest.
Arguments:
- inputs: bfloat16 [2, 256, 65536], P(None, None, 'neuron'), may hold values from -6 to 6
- weights: bfloat16 [16, 512, 3, 128, 128], P('section', 'neuron'), may hold values from -0.4375 to 0.4375
- bias: bfloat16 [16, 65536], P('section', 'neuron'), may hold values from -0.19921875 to 0.19921875
- offsets: int32 [16, 3], P('section'), may hold values from -3 to 3, as said below
Outputs:
- outputs: bfloat16 [2, 256, 65536], P(None, 'section', 'neuron')
The draws below stay inside these ranges and needn't reach their ends.
Inputs may be any that keep to these rules, and one draw needn't show every extreme that they name: `offsets`: band 0 has offset 0; band 1 lies in 1 .. 3 and band 2 in -3 .. -1; some layer has 3 in band 1 and some layer -3 in band 2.
All inputs are finite; a program needn't handle non-finite values.
Results may differ from the reference program's by a relative error of at most 0.029.
Values may be sent and summed in bfloat16 or wider, within the bound.
A program may use at most 128 MiB of HBM per device.

```python
import jax
import jax.numpy as jnp
from jax import lax

BLOCK = 128
BANDS = 3
HALO = 3
MICRO = 2
ROWS = 256
NBLOCKS = 512
NEURONS = 65536
LAYERS = 16


def draw_offsets(key, part):
    key_upward = jax.random.fold_in(key, 11)
    key_downward = jax.random.fold_in(key, 12)
    key_chosen = jax.random.fold_in(key, 13)
    upward = jax.random.randint(key_upward, (LAYERS,), 1, HALO + 1)
    downward = 0 - jax.random.randint(key_downward, (LAYERS,), 1, HALO + 1)
    chosen = jax.random.randint(key_chosen, (2,), 0, LAYERS)
    upward = upward.at[chosen[0]].set(HALO)
    downward = downward.at[chosen[1]].set(0 - HALO)
    center = jnp.zeros((LAYERS,), jnp.int32)
    return jnp.stack([center, upward.astype(jnp.int32), downward.astype(jnp.int32)], axis=1).astype(jnp.int32)


def levels(own_key, extent, shards, low, top_value):
    gain, own = 1.0, jax.random.fold_in(own_key, 6)
    for position, blocks in shards:
        steps = jnp.exp(jax.random.uniform(jax.random.fold_in(own, position), (blocks,), jnp.float32, low / len(shards), top_value / len(shards)))
        gain = gain * jnp.repeat(steps, extent[position] // blocks).reshape([-1 if axis == position else 1 for axis in range(len(extent))])
    return gain


def gaussian(rng, dims, deviation, most, cuts=(), held_as=jnp.bfloat16):
    factor_of = levels(rng, dims, cuts, -0.22, 0.18) if cuts else 1.0
    drawn = jax.random.normal(rng, dims, jnp.float32) * deviation * factor_of
    return jnp.minimum(jnp.maximum(drawn, -most), most).astype(held_as)


def setup_inputs(seed: int = 0) -> dict:
    splits = jax.random.split(jax.random.key(seed), 5)
    return {
        "inputs": gaussian(splits[0], (MICRO, ROWS, NEURONS), 1.0, 6.0, ((2, 32),)),
        "weights": gaussian(splits[1], (LAYERS, NBLOCKS, BANDS, BLOCK, BLOCK), (BANDS * BLOCK // 2) ** -0.5, 0.4375, ((0, 8), (1, 32))),
        "bias": jnp.clip(jax.random.uniform(splits[2], (LAYERS, NEURONS), jnp.float32, -0.19921875, 0.19921875) * levels(splits[2], (LAYERS, NEURONS), ((0, 8), (1, 32)), -0.4, 0.0), -0.19921875, 0.19921875).astype(jnp.bfloat16),
        "offsets": draw_offsets(jax.random.fold_in(splits[4], 71), 0),
    }


ceiling = 2.0


def reference(inputs, weights, bias, offsets):
    current = inputs
    micro_count, row_count, neuron_count = inputs.shape
    block_count = neuron_count // BLOCK
    for layer in range(LAYERS):
        summed = jnp.zeros((micro_count, row_count, block_count, BLOCK), jnp.float32)
        for band_index in range(BANDS):
            amount = (0 - offsets[layer, band_index] * BLOCK).astype(jnp.int32)
            moved = jnp.roll(current, amount, axis=2).reshape(micro_count, row_count, block_count, BLOCK).astype(jnp.float32)
            block_weights = weights[layer, :, band_index].astype(jnp.float32)
            summed = summed + jnp.einsum("mrjk,jkn->mrjn", moved, block_weights, precision=lax.Precision.HIGHEST)
        preact = summed.reshape(micro_count, row_count, neuron_count) + bias[layer].astype(jnp.float32)
        current = jnp.clip(preact, 0.0, ceiling).astype(jnp.bfloat16)
    return current
```

```python
import functools

import jax
import jax.numpy as jnp
from jax import lax
from jax.experimental import pallas as pl
from jax.experimental.pallas import tpu as pltpu
from jax.sharding import PartitionSpec as P

MESH = pl.DeviceIdType.MESH
HALO = 3
ceiling = 2.0
ROWS = 16
AHEAD = 2


def kernel(
    dims, offs, x, w, bias, out,
    wa, wb, bl, br, bs, zin, zout, hl, hr, work, mid,
    zs, zr, ls, lr, rs, rr, og, ws, wr,
):
    sections, devices, micro, share, chunks, blocks, size = dims
    rows = ROWS
    width = 2 * HALO * size
    sec = lax.axis_index("section")
    me = lax.axis_index("neuron")
    left = lax.rem(me + devices - 1, devices)
    right = lax.rem(me + 1, devices)
    after = lax.rem(sec + 1, sections)
    before = lax.rem(sec + sections - 1, sections)
    per_share = share // rows
    per_owner = micro * per_share

    barrier = pltpu.get_barrier_semaphore()
    for where in ({"neuron": left}, {"neuron": right}, {"section": after}, {"section": before}):
        pl.semaphore_signal(barrier, inc=1, device_id=where, device_id_type=MESH)

    def place(c):
        owner = c // per_owner
        slot = c % per_owner
        batch = slot // per_share
        row = (slot % per_share) * rows
        return owner, slot, batch, row

    def fetch(c):
        owner, _, batch, row = place(c)
        start = pl.multiple_of(owner * share + row, rows)
        return pltpu.make_async_copy(x.at[batch, pl.ds(start, rows), :], zin.at[c], zr.at[c])

    def forward(c):
        return pltpu.make_async_remote_copy(
            src_ref=zout.at[c], dst_ref=zin.at[c], send_sem=zs.at[c], recv_sem=zr.at[c],
            device_id={"section": after}, device_id_type=MESH)

    def deliver(c):
        owner, slot, batch, row = place(c)
        target = out.at[batch, pl.ds(pl.multiple_of(row, rows), rows), :]
        return pltpu.make_async_remote_copy(
            src_ref=zout.at[c], dst_ref=target, send_sem=zs.at[c], recv_sem=og.at[slot],
            device_id={"section": owner}, device_id_type=MESH)

    def keep(c):
        _, _, batch, row = place(c)
        target = out.at[batch, pl.ds(pl.multiple_of(row, rows), rows), :]
        return pltpu.make_async_copy(zout.at[c], target, zs.at[c])

    def to_left(c):
        return pltpu.make_async_remote_copy(
            src_ref=zin.at[c, :, pl.ds(0, width)], dst_ref=hr.at[c], send_sem=ls.at[c], recv_sem=rr.at[c],
            device_id={"neuron": left}, device_id_type=MESH)

    def to_right(c):
        return pltpu.make_async_remote_copy(
            src_ref=zin.at[c, :, pl.ds(blocks * size - width, width)], dst_ref=hl.at[c],
            send_sem=rs.at[c], recv_sem=lr.at[c],
            device_id={"neuron": right}, device_id_type=MESH)

    first = sec == 0
    last = sec == sections - 1

    @pl.when(first)
    def _():
        @pl.loop(0, chunks)
        def _(c):
            fetch(c).start()

    own_a = pltpu.make_async_copy(w.at[0], wa.at[pl.ds(HALO, blocks)], ws.at[0])
    own_b = pltpu.make_async_copy(w.at[1], wb, ws.at[1])
    own_a.start()
    own_b.start()
    pl.semaphore_wait(barrier, 4)

    def receive(c):
        @pl.when(first)
        def _():
            fetch(c).wait()

        @pl.when(jnp.logical_not(first))
        def _():
            forward(c).wait_recv()

        to_left(c).start()
        to_right(c).start()

    edge_left = pltpu.make_async_remote_copy(
        src_ref=w.at[0, pl.ds(0, HALO)], dst_ref=wa.at[pl.ds(HALO + blocks, HALO)],
        send_sem=ws.at[2], recv_sem=wr.at[0], device_id={"neuron": left}, device_id_type=MESH)
    edge_right = pltpu.make_async_remote_copy(
        src_ref=w.at[0, pl.ds(blocks - HALO, HALO)], dst_ref=wa.at[pl.ds(0, HALO)],
        send_sem=ws.at[3], recv_sem=wr.at[1], device_id={"neuron": right}, device_id_type=MESH)
    bias_left = pltpu.make_async_remote_copy(
        src_ref=bias.at[:, pl.ds(0, HALO * size)], dst_ref=br,
        send_sem=ws.at[4], recv_sem=wr.at[2], device_id={"neuron": left}, device_id_type=MESH)
    bias_right = pltpu.make_async_remote_copy(
        src_ref=bias.at[:, pl.ds((blocks - HALO) * size, HALO * size)], dst_ref=bl,
        send_sem=ws.at[5], recv_sem=wr.at[3], device_id={"neuron": right}, device_id_type=MESH)
    edges = (bias_left, bias_right, edge_left, edge_right)
    for copy in edges:
        copy.start()
    for c in range(AHEAD):
        @pl.when(first)
        def _(c=c):
            receive(c)
    for copy in (bias_left, bias_right):
        copy.wait()
    span = blocks + 2 * HALO
    own = bias[...].astype(jnp.float32)
    from_left = bl[...].astype(jnp.float32)
    from_right = br[...].astype(jnp.float32)
    for j in range(HALO):
        bs[j : j + 1, :] = from_left[0:1, j * size : (j + 1) * size]
        bs[HALO + blocks + j : HALO + blocks + j + 1, :] = from_right[0:1, j * size : (j + 1) * size]
    for j in range(blocks):
        bs[HALO + j : HALO + j + 1, :] = own[0:1, j * size : (j + 1) * size]
        bs[span + j : span + j + 1, :] = own[1:2, j * size : (j + 1) * size]
    own_a.wait()
    own_b.wait()
    edge_left.wait()
    edge_right.wait()
    for c in range(AHEAD):
        @pl.when(jnp.logical_not(first))
        def _(c=c):
            receive(c)

    def apply(source, weights, j, shift, bias_row):
        taken = [source[j + s] for s in shift]
        joined = jnp.concatenate(taken, axis=1)
        total = jnp.dot(joined, weights[j].reshape(len(shift) * size, size), preferred_element_type=jnp.float32)
        total = total + bs[bias_row : bias_row + 1, :]
        return jnp.minimum(jnp.maximum(total, 0.0), ceiling).astype(jnp.bfloat16)

    bands = w.shape[2]
    shift_a = [offs[0, b] + HALO for b in range(bands)]
    shift_b = [offs[1, b] + HALO for b in range(bands)]

    @pl.loop(0, chunks)
    def _(c):
        @pl.when(c + AHEAD < chunks)
        def _():
            receive(c + AHEAD)

        for j in range(blocks):
            work[2 * HALO + j] = zin[c, :, j * size : (j + 1) * size]
        to_left(c).wait_recv()
        for j in range(2 * HALO):
            work[2 * HALO + blocks + j] = hr[c, :, j * size : (j + 1) * size]
        to_right(c).wait_recv()
        for j in range(2 * HALO):
            work[j] = hl[c, :, j * size : (j + 1) * size]
        for j in range(span):
            mid[j] = apply(work, wa, j, shift_a, j)
        for j in range(blocks):
            zout[c, :, j * size : (j + 1) * size] = apply(mid, wb, j, shift_b, span + j)

        @pl.when(jnp.logical_not(last))
        def _():
            forward(c).start()

        @pl.when(last)
        def _():
            @pl.when(c // per_owner < sections - 1)
            def _():
                deliver(c).start()

            @pl.when(c // per_owner == sections - 1)
            def _():
                keep(c).start()

    @pl.loop(0, chunks)
    def _(c):
        to_left(c).wait_send()
        to_right(c).wait_send()

        @pl.when(jnp.logical_not(last))
        def _():
            forward(c).wait_send()

        @pl.when(last)
        def _():
            @pl.when(c // per_owner < sections - 1)
            def _():
                deliver(c).wait_send()

            @pl.when(c // per_owner == sections - 1)
            def _():
                keep(c).wait()

    @pl.when(jnp.logical_not(last))
    def _():
        @pl.loop(0, per_owner)
        def _(c):
            deliver(c).wait_recv()


def shards(sections, devices, inputs, weights, bias, offsets):
    micro, row_count, local = inputs.shape
    layers, blocks, bands, size = weights.shape[:4]
    share = row_count // sections
    chunks = micro * row_count // ROWS
    span = blocks + 2 * HALO
    bf16, dma = jnp.bfloat16, pltpu.SemaphoreType.DMA
    dims = (sections, devices, micro, share, chunks, blocks, size)
    return pl.pallas_call(
        functools.partial(kernel, dims),
        out_shape=jax.ShapeDtypeStruct((micro, share, local), bf16),
        in_specs=[
            pl.BlockSpec(memory_space=pltpu.SMEM),
            pl.BlockSpec(memory_space=pl.ANY),
            pl.BlockSpec(memory_space=pl.ANY),
            pl.BlockSpec(memory_space=pltpu.VMEM),
        ],
        out_specs=pl.BlockSpec(memory_space=pl.ANY),
        scratch_shapes=[
            pltpu.VMEM((span, bands, size, size), bf16),
            pltpu.VMEM((blocks, bands, size, size), bf16),
            pltpu.VMEM((layers, HALO * size), bf16),
            pltpu.VMEM((layers, HALO * size), bf16),
            pltpu.VMEM((span + blocks + 2, size), jnp.float32),
            pltpu.VMEM((chunks, ROWS, local), bf16),
            pltpu.VMEM((chunks, ROWS, local), bf16),
            pltpu.VMEM((chunks, ROWS, 2 * HALO * size), bf16),
            pltpu.VMEM((chunks, ROWS, 2 * HALO * size), bf16),
            pltpu.VMEM((span + 2 * HALO, ROWS, size), bf16),
            pltpu.VMEM((span, ROWS, size), bf16),
            dma((chunks,)), dma((chunks,)), dma((chunks,)), dma((chunks,)), dma((chunks,)), dma((chunks,)),
            dma((micro * share // ROWS,)), dma((6,)), dma((4,)),
        ],
        compiler_params=pltpu.CompilerParams(collective_id=0, has_side_effects=True),
    )(offsets, inputs, weights, bias)


def solution(mesh):
    in_specs = (
        P(None, None, "neuron"),
        P("section", "neuron", None, None, None),
        P("section", "neuron"),
        P("section", None),
    )
    out_specs = P(None, "section", "neuron")
    body = functools.partial(shards, mesh.shape["section"], mesh.shape["neuron"])
    return jax.shard_map(body, mesh=mesh, in_specs=in_specs, out_specs=out_specs, check_vma=False)
```

```python
import functools

import jax
import jax.numpy as jnp
from jax import lax
from jax.experimental import pallas as pl
from jax.experimental.pallas import tpu as pltpu
from jax.sharding import PartitionSpec as P

MESH = pl.DeviceIdType.MESH
HALO = 3
ceiling = 2.0
ROWS = 16
AHEAD = 3


def kernel(
    dims, offs, x, w, bias, out,
    wa, wb, bl, br, bs, zin, zout, hl, hr, work, mid_low, mid_high,
    zs, zr, ls, lr, rs, rr, og, ws, wr,
):
    sections, devices, micro, share, chunks, blocks, size = dims
    rows = ROWS
    width = 2 * HALO * size
    sec = lax.axis_index("section")
    me = lax.axis_index("neuron")
    left = lax.rem(me + devices - 1, devices)
    right = lax.rem(me + 1, devices)
    after = lax.rem(sec + 1, sections)
    before = lax.rem(sec + sections - 1, sections)
    per_share = share // rows
    per_owner = micro * per_share

    barrier = pltpu.get_barrier_semaphore()
    first = sec == 0
    last = sec == sections - 1
    for where in ({"neuron": left}, {"neuron": right}):
        pl.semaphore_signal(barrier, inc=1, device_id=where, device_id_type=MESH)

    @pl.when(jnp.logical_not(last))
    def _():
        pl.semaphore_signal(barrier, inc=1, device_id={"section": after}, device_id_type=MESH)

    @pl.when(jnp.logical_not(first))
    def _():
        pl.semaphore_signal(barrier, inc=1, device_id={"section": before}, device_id_type=MESH)

    def place(c):
        owner = c // per_owner
        slot = c % per_owner
        batch = slot // per_share
        row = (slot % per_share) * rows
        return owner, slot, batch, row

    def fetch(c):
        owner, _, batch, row = place(c)
        start = pl.multiple_of(owner * share + row, rows)
        return pltpu.make_async_copy(x.at[batch, pl.ds(start, rows), :], zin.at[c], zr.at[c])

    def forward(c):
        return pltpu.make_async_remote_copy(
            src_ref=zout.at[c], dst_ref=zin.at[c], send_sem=zs.at[c], recv_sem=zr.at[c],
            device_id={"section": after}, device_id_type=MESH)

    def deliver(c):
        owner, slot, batch, row = place(c)
        target = out.at[batch, pl.ds(pl.multiple_of(row, rows), rows), :]
        return pltpu.make_async_remote_copy(
            src_ref=zout.at[c], dst_ref=target, send_sem=zs.at[c], recv_sem=og.at[slot],
            device_id={"section": owner}, device_id_type=MESH)

    def keep(c):
        _, _, batch, row = place(c)
        target = out.at[batch, pl.ds(pl.multiple_of(row, rows), rows), :]
        return pltpu.make_async_copy(zout.at[c], target, zs.at[c])

    def to_left(c):
        return pltpu.make_async_remote_copy(
            src_ref=zin.at[c, :, pl.ds(0, width)], dst_ref=hr.at[c], send_sem=ls.at[c], recv_sem=rr.at[c],
            device_id={"neuron": left}, device_id_type=MESH)

    def to_right(c):
        return pltpu.make_async_remote_copy(
            src_ref=zin.at[c, :, pl.ds(blocks * size - width, width)], dst_ref=hl.at[c],
            send_sem=rs.at[c], recv_sem=lr.at[c],
            device_id={"neuron": right}, device_id_type=MESH)

    @pl.when(first)
    def _():
        for c in range(AHEAD):
            fetch(c).start()

    own_a = pltpu.make_async_copy(w.at[0], wa.at[pl.ds(HALO, blocks)], ws.at[0])
    own_b = pltpu.make_async_copy(w.at[1], wb, ws.at[1])
    own_a.start()
    own_b.start()

    @pl.when(first)
    def _():
        @pl.loop(AHEAD, chunks)
        def _(c):
            fetch(c).start()

    @pl.when(jnp.logical_or(first, last))
    def _():
        pl.semaphore_wait(barrier, 3)

    @pl.when(jnp.logical_not(jnp.logical_or(first, last)))
    def _():
        pl.semaphore_wait(barrier, 4)


    def receive(c):
        @pl.when(first)
        def _():
            fetch(c).wait()

        @pl.when(jnp.logical_not(first))
        def _():
            forward(c).wait_recv()

        to_left(c).start()
        to_right(c).start()

    edge_left = pltpu.make_async_remote_copy(
        src_ref=w.at[0, pl.ds(0, HALO)], dst_ref=wa.at[pl.ds(HALO + blocks, HALO)],
        send_sem=ws.at[2], recv_sem=wr.at[0], device_id={"neuron": left}, device_id_type=MESH)
    edge_right = pltpu.make_async_remote_copy(
        src_ref=w.at[0, pl.ds(blocks - HALO, HALO)], dst_ref=wa.at[pl.ds(0, HALO)],
        send_sem=ws.at[3], recv_sem=wr.at[1], device_id={"neuron": right}, device_id_type=MESH)
    bias_left = pltpu.make_async_remote_copy(
        src_ref=bias.at[:, pl.ds(0, HALO * size)], dst_ref=br,
        send_sem=ws.at[4], recv_sem=wr.at[2], device_id={"neuron": left}, device_id_type=MESH)
    bias_right = pltpu.make_async_remote_copy(
        src_ref=bias.at[:, pl.ds((blocks - HALO) * size, HALO * size)], dst_ref=bl,
        send_sem=ws.at[5], recv_sem=wr.at[3], device_id={"neuron": right}, device_id_type=MESH)
    edges = (bias_left, bias_right, edge_left, edge_right)
    for copy in edges:
        copy.start()
    for c in range(AHEAD):
        @pl.when(first)
        def _(c=c):
            receive(c)
    for copy in (bias_left, bias_right):
        copy.wait()
    span = blocks + 2 * HALO
    own = bias[...].astype(jnp.float32)
    from_left = bl[...].astype(jnp.float32)
    from_right = br[...].astype(jnp.float32)
    for j in range(HALO):
        bs[j : j + 1, :] = from_left[0:1, j * size : (j + 1) * size]
        bs[HALO + blocks + j : HALO + blocks + j + 1, :] = from_right[0:1, j * size : (j + 1) * size]
    for j in range(blocks):
        bs[HALO + j : HALO + j + 1, :] = own[0:1, j * size : (j + 1) * size]
        bs[span + j : span + j + 1, :] = own[1:2, j * size : (j + 1) * size]
    own_a.wait()
    own_b.wait()
    edge_left.wait()
    edge_right.wait()
    for c in range(AHEAD):
        @pl.when(jnp.logical_not(first))
        def _(c=c):
            receive(c)

    def apply(source, weights, j, at, shift, bias_row):
        low = [jnp.concatenate([source[at + k + s] for s in shift[:2]], axis=1) for k in range(2)]
        sums = [
            jnp.dot(low[k], weights[j + k, 0:2].reshape(2 * size, size), preferred_element_type=jnp.float32)
            for k in range(2)
        ]
        zero = jnp.zeros((rows, size), jnp.bfloat16)
        third = jnp.concatenate(
            [
                jnp.concatenate([source[at + shift[2]], zero], axis=1),
                jnp.concatenate([zero, source[at + 1 + shift[2]]], axis=1),
            ],
            axis=0,
        )
        both = jnp.concatenate([weights[j, 2], weights[j + 1, 2]], axis=0)
        rest = jnp.dot(third, both, preferred_element_type=jnp.float32)
        done = []
        for k in range(2):
            total = sums[k] + rest[k * rows : (k + 1) * rows] + bs[bias_row + k : bias_row + k + 1, :]
            done.append(jnp.minimum(jnp.maximum(total, 0.0), ceiling).astype(jnp.bfloat16))
        return done

    bands = w.shape[2]
    shift_a = [offs[0, b] + HALO for b in range(bands)]
    shift_b = [offs[1, b] + HALO for b in range(bands)]

    @pl.loop(0, chunks)
    def _(c):
        @pl.when(c + AHEAD < chunks)
        def _():
            receive(c + AHEAD)

        for j in range(blocks):
            work[2 * HALO + j] = zin[c, :, j * size : (j + 1) * size]
        to_left(c).wait_recv()
        for j in range(2 * HALO):
            work[2 * HALO + blocks + j] = hr[c, :, j * size : (j + 1) * size]
        to_right(c).wait_recv()
        for j in range(2 * HALO):
            work[j] = hl[c, :, j * size : (j + 1) * size]
        half = blocks // 2
        for j in range(0, span, 2):
            for k, block in enumerate(apply(work, wa, j, j, shift_a, j)):
                if j + k < half + 2 * HALO:
                    mid_low[j + k] = block
                if j + k >= half:
                    mid_high[j + k - half] = block
        for j in range(0, blocks, 2):
            source, at = (mid_low, j) if j < half else (mid_high, j - half)
            for k, block in enumerate(apply(source, wb, j, at, shift_b, span + j)):
                zout[c, :, (j + k) * size : (j + k + 1) * size] = block

        @pl.when(jnp.logical_not(last))
        def _():
            forward(c).start()

        @pl.when(last)
        def _():
            @pl.when(c // per_owner < sections - 1)
            def _():
                deliver(c).start()

            @pl.when(c // per_owner == sections - 1)
            def _():
                keep(c).start()

    @pl.loop(0, chunks)
    def _(c):
        to_left(c).wait_send()
        to_right(c).wait_send()

        @pl.when(jnp.logical_not(last))
        def _():
            forward(c).wait_send()

        @pl.when(last)
        def _():
            @pl.when(c // per_owner < sections - 1)
            def _():
                deliver(c).wait_send()

            @pl.when(c // per_owner == sections - 1)
            def _():
                keep(c).wait()

    @pl.when(jnp.logical_not(last))
    def _():
        @pl.loop(0, per_owner)
        def _(c):
            deliver(c).wait_recv()


def shards(sections, devices, inputs, weights, bias, offsets):
    micro, row_count, local = inputs.shape
    layers, blocks, bands, size = weights.shape[:4]
    share = row_count // sections
    chunks = micro * row_count // ROWS
    span = blocks + 2 * HALO
    bf16, dma = jnp.bfloat16, pltpu.SemaphoreType.DMA
    dims = (sections, devices, micro, share, chunks, blocks, size)
    return pl.pallas_call(
        functools.partial(kernel, dims),
        out_shape=jax.ShapeDtypeStruct((micro, share, local), bf16),
        in_specs=[
            pl.BlockSpec(memory_space=pltpu.SMEM),
            pl.BlockSpec(memory_space=pl.ANY),
            pl.BlockSpec(memory_space=pl.ANY),
            pl.BlockSpec(memory_space=pltpu.VMEM),
        ],
        out_specs=pl.BlockSpec(memory_space=pl.ANY),
        scratch_shapes=[
            pltpu.VMEM((span, bands, size, size), bf16),
            pltpu.VMEM((blocks, bands, size, size), bf16),
            pltpu.VMEM((layers, HALO * size), bf16),
            pltpu.VMEM((layers, HALO * size), bf16),
            pltpu.VMEM((span + blocks + 2, size), jnp.float32),
            pltpu.VMEM((chunks, ROWS, local), bf16),
            pltpu.VMEM((chunks, ROWS, local), bf16),
            pltpu.VMEM((chunks, ROWS, 2 * HALO * size), bf16),
            pltpu.VMEM((chunks, ROWS, 2 * HALO * size), bf16),
            pltpu.VMEM((span + 2 * HALO, ROWS, size), bf16),
            pltpu.VMEM((blocks // 2 + 2 * HALO, ROWS, size), bf16),
            pltpu.VMEM((blocks // 2 + 2 * HALO, ROWS, size), bf16),
            dma((chunks,)), dma((chunks,)), dma((chunks,)), dma((chunks,)), dma((chunks,)), dma((chunks,)),
            dma((micro * share // ROWS,)), dma((6,)), dma((4,)),
        ],
        compiler_params=pltpu.CompilerParams(collective_id=0, has_side_effects=True),
    )(offsets, inputs, weights, bias)


def solution(mesh):
    in_specs = (
        P(None, None, "neuron"),
        P("section", "neuron", None, None, None),
        P("section", "neuron"),
        P("section", None),
    )
    out_specs = P(None, "section", "neuron")
    body = functools.partial(shards, mesh.shape["section"], mesh.shape["neuron"])
    return jax.shard_map(body, mesh=mesh, in_specs=in_specs, out_specs=out_specs, check_vma=False)
```

```python
import functools

import jax
import jax.numpy as jnp
from jax import lax
from jax.experimental import pallas as pl
from jax.experimental.pallas import tpu as pltpu
from jax.sharding import PartitionSpec as P

MESH = pl.DeviceIdType.MESH
HALO = 3
ceiling = 2.0
ROWS = 16
OUTER = 3
INNER = 2


def kernel(
    dims, offs, x, w, bias, out,
    wa, wb, bl, br, bs, zin, zout, ho, hi, work, mid_low, mid_high,
    es, er, zs, zr, os, orr, ks, kr, og, ws, wr,
):
    sections, devices, micro, share, chunks, blocks, size = dims
    rows = ROWS
    width = 2 * HALO * size
    sec = lax.axis_index("section")
    me = lax.axis_index("neuron")
    left = lax.rem(me + devices - 1, devices)
    right = lax.rem(me + 1, devices)
    after = lax.rem(sec + 1, sections)
    before = lax.rem(sec + sections - 1, sections)
    per_share = share // rows
    per_owner = micro * per_share

    barrier = pltpu.get_barrier_semaphore()
    first = sec == 0
    last = sec == sections - 1
    for where in ({"neuron": left}, {"neuron": right}):
        pl.semaphore_signal(barrier, inc=1, device_id=where, device_id_type=MESH)

    @pl.when(jnp.logical_not(last))
    def _():
        pl.semaphore_signal(barrier, inc=1, device_id={"section": after}, device_id_type=MESH)

    @pl.when(jnp.logical_not(first))
    def _():
        pl.semaphore_signal(barrier, inc=1, device_id={"section": before}, device_id_type=MESH)

    def place(c):
        owner = c // per_owner
        slot = c % per_owner
        batch = slot // per_share
        row = (slot % per_share) * rows
        return owner, slot, batch, row

    def fetch(c):
        owner, _, batch, row = place(c)
        start = pl.multiple_of(owner * share + row, rows)
        return pltpu.make_async_copy(x.at[batch, pl.ds(start, rows), :], zin.at[c], er.at[c])

    odd = lax.rem(me, 2)
    outer = lax.rem(me + devices - 1 + 2 * odd, devices)
    inner = me + 1 - 2 * odd
    rest = blocks * size - width
    outer_start = pl.multiple_of(odd * rest, size)
    inner_start = pl.multiple_of((1 - odd) * rest, size)
    rest_start = pl.multiple_of((1 - odd) * width, size)

    def forward_edge(c):
        cut = pl.ds(outer_start, width)
        return pltpu.make_async_remote_copy(
            src_ref=zout.at[c, :, cut], dst_ref=zin.at[c, :, cut], send_sem=es.at[c], recv_sem=er.at[c],
            device_id={"section": after}, device_id_type=MESH)

    def forward(c):
        cut = pl.ds(rest_start, rest)
        return pltpu.make_async_remote_copy(
            src_ref=zout.at[c, :, cut], dst_ref=zin.at[c, :, cut], send_sem=zs.at[c], recv_sem=zr.at[c],
            device_id={"section": after}, device_id_type=MESH)

    def deliver(c):
        owner, slot, batch, row = place(c)
        target = out.at[batch, pl.ds(pl.multiple_of(row, rows), rows), :]
        return pltpu.make_async_remote_copy(
            src_ref=zout.at[c], dst_ref=target, send_sem=zs.at[c], recv_sem=og.at[slot],
            device_id={"section": owner}, device_id_type=MESH)

    def keep(c):
        _, _, batch, row = place(c)
        target = out.at[batch, pl.ds(pl.multiple_of(row, rows), rows), :]
        return pltpu.make_async_copy(zout.at[c], target, zs.at[c])

    def to_outer(c):
        return pltpu.make_async_remote_copy(
            src_ref=zin.at[c, :, pl.ds(outer_start, width)], dst_ref=ho.at[c], send_sem=os.at[c], recv_sem=orr.at[c],
            device_id={"neuron": outer}, device_id_type=MESH)

    def to_inner(c):
        return pltpu.make_async_remote_copy(
            src_ref=zin.at[c, :, pl.ds(inner_start, width)], dst_ref=hi.at[c], send_sem=ks.at[c], recv_sem=kr.at[c],
            device_id={"neuron": inner}, device_id_type=MESH)

    @pl.when(first)
    def _():
        for c in range(OUTER):
            fetch(c).start()

    own_a = pltpu.make_async_copy(w.at[0], wa.at[pl.ds(HALO, blocks)], ws.at[0])
    own_b = pltpu.make_async_copy(w.at[1], wb, ws.at[1])
    own_a.start()
    own_b.start()

    @pl.when(first)
    def _():
        @pl.loop(OUTER, chunks)
        def _(c):
            fetch(c).start()

    @pl.when(jnp.logical_or(first, last))
    def _():
        pl.semaphore_wait(barrier, 3)

    @pl.when(jnp.logical_not(jnp.logical_or(first, last)))
    def _():
        pl.semaphore_wait(barrier, 4)


    def receive_outer(c):
        @pl.when(first)
        def _():
            fetch(c).wait()

        @pl.when(jnp.logical_not(first))
        def _():
            forward_edge(c).wait_recv()

        to_outer(c).start()

    def receive_inner(c):
        @pl.when(jnp.logical_not(first))
        def _():
            forward(c).wait_recv()

        to_inner(c).start()

    def receive_first():
        for c in range(OUTER):
            receive_outer(c)
            if c < INNER:
                receive_inner(c)

    edge_left = pltpu.make_async_remote_copy(
        src_ref=w.at[0, pl.ds(0, HALO)], dst_ref=wa.at[pl.ds(HALO + blocks, HALO)],
        send_sem=ws.at[2], recv_sem=wr.at[0], device_id={"neuron": left}, device_id_type=MESH)
    edge_right = pltpu.make_async_remote_copy(
        src_ref=w.at[0, pl.ds(blocks - HALO, HALO)], dst_ref=wa.at[pl.ds(0, HALO)],
        send_sem=ws.at[3], recv_sem=wr.at[1], device_id={"neuron": right}, device_id_type=MESH)
    bias_left = pltpu.make_async_remote_copy(
        src_ref=bias.at[:, pl.ds(0, HALO * size)], dst_ref=br,
        send_sem=ws.at[4], recv_sem=wr.at[2], device_id={"neuron": left}, device_id_type=MESH)
    bias_right = pltpu.make_async_remote_copy(
        src_ref=bias.at[:, pl.ds((blocks - HALO) * size, HALO * size)], dst_ref=bl,
        send_sem=ws.at[5], recv_sem=wr.at[3], device_id={"neuron": right}, device_id_type=MESH)
    edges = (bias_left, bias_right, edge_left, edge_right)
    for copy in edges:
        copy.start()

    @pl.when(first)
    def _():
        receive_first()

    for copy in (bias_left, bias_right):
        copy.wait()
    span = blocks + 2 * HALO
    own = bias[...].astype(jnp.float32)
    from_left = bl[...].astype(jnp.float32)
    from_right = br[...].astype(jnp.float32)
    for j in range(HALO):
        bs[j : j + 1, :] = from_left[0:1, j * size : (j + 1) * size]
        bs[HALO + blocks + j : HALO + blocks + j + 1, :] = from_right[0:1, j * size : (j + 1) * size]
    for j in range(blocks):
        bs[HALO + j : HALO + j + 1, :] = own[0:1, j * size : (j + 1) * size]
        bs[span + j : span + j + 1, :] = own[1:2, j * size : (j + 1) * size]
    own_a.wait()
    own_b.wait()
    edge_left.wait()
    edge_right.wait()

    @pl.when(jnp.logical_not(first))
    def _():
        receive_first()

    def apply(source, weights, j, at, shift, bias_row):
        low = [jnp.concatenate([source[at + k + s] for s in shift[:2]], axis=1) for k in range(2)]
        sums = [
            jnp.dot(low[k], weights[j + k, 0:2].reshape(2 * size, size), preferred_element_type=jnp.float32)
            for k in range(2)
        ]
        zero = jnp.zeros((rows, size), jnp.bfloat16)
        third = jnp.concatenate(
            [
                jnp.concatenate([source[at + shift[2]], zero], axis=1),
                jnp.concatenate([zero, source[at + 1 + shift[2]]], axis=1),
            ],
            axis=0,
        )
        both = jnp.concatenate([weights[j, 2], weights[j + 1, 2]], axis=0)
        rest = jnp.dot(third, both, preferred_element_type=jnp.float32)
        done = []
        for k in range(2):
            total = sums[k] + rest[k * rows : (k + 1) * rows] + bs[bias_row + k : bias_row + k + 1, :]
            done.append(jnp.minimum(jnp.maximum(total, 0.0), ceiling).astype(jnp.bfloat16))
        return done

    bands = w.shape[2]
    outer_base = odd * (2 * HALO + blocks)
    inner_base = (1 - odd) * (2 * HALO + blocks)
    shift_a = [offs[0, b] + HALO for b in range(bands)]
    shift_b = [offs[1, b] + HALO for b in range(bands)]

    @pl.loop(0, chunks)
    def _(c):
        @pl.when(c + INNER < chunks)
        def _():
            receive_inner(c + INNER)

        @pl.when(c + OUTER < chunks)
        def _():
            receive_outer(c + OUTER)

        for j in range(blocks):
            work[2 * HALO + j] = zin[c, :, j * size : (j + 1) * size]
        to_inner(c).wait_recv()
        for j in range(2 * HALO):
            work[inner_base + j] = hi[c, :, j * size : (j + 1) * size]
        to_outer(c).wait_recv()
        for j in range(2 * HALO):
            work[outer_base + j] = ho[c, :, j * size : (j + 1) * size]
        half = blocks // 2
        for j in range(0, span, 2):
            for k, block in enumerate(apply(work, wa, j, j, shift_a, j)):
                if j + k < half + 2 * HALO:
                    mid_low[j + k] = block
                if j + k >= half:
                    mid_high[j + k - half] = block
        for j in range(0, blocks, 2):
            source, at = (mid_low, j) if j < half else (mid_high, j - half)
            for k, block in enumerate(apply(source, wb, j, at, shift_b, span + j)):
                zout[c, :, (j + k) * size : (j + k + 1) * size] = block

        @pl.when(jnp.logical_not(last))
        def _():
            forward_edge(c).start()
            forward(c).start()

        @pl.when(last)
        def _():
            @pl.when(c // per_owner < sections - 1)
            def _():
                deliver(c).start()

            @pl.when(c // per_owner == sections - 1)
            def _():
                keep(c).start()

    @pl.loop(0, chunks)
    def _(c):
        to_outer(c).wait_send()
        to_inner(c).wait_send()

        @pl.when(jnp.logical_not(last))
        def _():
            forward_edge(c).wait_send()
            forward(c).wait_send()

        @pl.when(last)
        def _():
            @pl.when(c // per_owner < sections - 1)
            def _():
                deliver(c).wait_send()

            @pl.when(c // per_owner == sections - 1)
            def _():
                keep(c).wait()

    @pl.when(jnp.logical_not(last))
    def _():
        @pl.loop(0, per_owner)
        def _(c):
            deliver(c).wait_recv()


def shards(sections, devices, inputs, weights, bias, offsets):
    micro, row_count, local = inputs.shape
    layers, blocks, bands, size = weights.shape[:4]
    share = row_count // sections
    chunks = micro * row_count // ROWS
    span = blocks + 2 * HALO
    bf16, dma = jnp.bfloat16, pltpu.SemaphoreType.DMA
    dims = (sections, devices, micro, share, chunks, blocks, size)
    return pl.pallas_call(
        functools.partial(kernel, dims),
        out_shape=jax.ShapeDtypeStruct((micro, share, local), bf16),
        in_specs=[
            pl.BlockSpec(memory_space=pltpu.SMEM),
            pl.BlockSpec(memory_space=pl.ANY),
            pl.BlockSpec(memory_space=pl.ANY),
            pl.BlockSpec(memory_space=pltpu.VMEM),
        ],
        out_specs=pl.BlockSpec(memory_space=pl.ANY),
        scratch_shapes=[
            pltpu.VMEM((span, bands, size, size), bf16),
            pltpu.VMEM((blocks, bands, size, size), bf16),
            pltpu.VMEM((layers, HALO * size), bf16),
            pltpu.VMEM((layers, HALO * size), bf16),
            pltpu.VMEM((span + blocks + 2, size), jnp.float32),
            pltpu.VMEM((chunks, ROWS, local), bf16),
            pltpu.VMEM((chunks, ROWS, local), bf16),
            pltpu.VMEM((chunks, ROWS, 2 * HALO * size), bf16),
            pltpu.VMEM((chunks, ROWS, 2 * HALO * size), bf16),
            pltpu.VMEM((span + 2 * HALO, ROWS, size), bf16),
            pltpu.VMEM((blocks // 2 + 2 * HALO, ROWS, size), bf16),
            pltpu.VMEM((blocks // 2 + 2 * HALO, ROWS, size), bf16),
            *[dma((chunks,))] * 8,
            dma((micro * share // ROWS,)), dma((6,)), dma((4,)),
        ],
        compiler_params=pltpu.CompilerParams(collective_id=0, has_side_effects=True),
    )(offsets, inputs, weights, bias)


def solution(mesh):
    in_specs = (
        P(None, None, "neuron"),
        P("section", "neuron", None, None, None),
        P("section", "neuron"),
        P("section", None),
    )
    out_specs = P(None, "section", "neuron")
    body = functools.partial(shards, mesh.shape["section"], mesh.shape["neuron"])
    return jax.shard_map(body, mesh=mesh, in_specs=in_specs, out_specs=out_specs, check_vma=False)
```

```python
import functools

import jax
import jax.numpy as jnp
from jax import lax
from jax.experimental import pallas as pl
from jax.experimental.pallas import tpu as pltpu
from jax.sharding import PartitionSpec as P

MESH = pl.DeviceIdType.MESH
HALO = 3
ceiling = 2.0
ROWS = 16
OUTER = 3
FIRST = 3
INNER = FIRST + 1
SLOTS = FIRST + 1


def kernel(
    dims, offs, x, w, bias, out,
    wa, wb, bo, bi, bs, zin, zout, ho, hi, work, mid,
    es, er, zs, zr, os, orr, ks, kr, og, ws, wr,
):
    sections, devices, micro, share, chunks, blocks, size = dims
    rows = ROWS
    width = 2 * HALO * size
    sec = lax.axis_index("section")
    me = lax.axis_index("neuron")
    left = lax.rem(me + devices - 1, devices)
    right = lax.rem(me + 1, devices)
    after = lax.rem(sec + 1, sections)
    before = lax.rem(sec + sections - 1, sections)
    per_share = share // rows
    per_owner = micro * per_share

    barrier = pltpu.get_barrier_semaphore()
    first = sec == 0
    last = sec == sections - 1
    for where in ({"neuron": left}, {"neuron": right}):
        pl.semaphore_signal(barrier, inc=1, device_id=where, device_id_type=MESH)

    @pl.when(jnp.logical_not(last))
    def _():
        pl.semaphore_signal(barrier, inc=1, device_id={"section": after}, device_id_type=MESH)

    @pl.when(jnp.logical_not(first))
    def _():
        pl.semaphore_signal(barrier, inc=1, device_id={"section": before}, device_id_type=MESH)

    def place(c):
        owner = c // per_owner
        slot = c % per_owner
        batch = slot // per_share
        row = (slot % per_share) * rows
        return owner, slot, batch, row

    def fetch(c):
        owner, _, batch, row = place(c)
        start = pl.multiple_of(owner * share + row, rows)
        return pltpu.make_async_copy(x.at[batch, pl.ds(start, rows), :], zin.at[c], er.at[c])

    odd = lax.rem(me, 2)
    outer = lax.rem(me + devices - 1 + 2 * odd, devices)
    inner = me + 1 - 2 * odd
    rest = blocks * size - width
    outer_start = pl.multiple_of(odd * rest, size)
    inner_start = pl.multiple_of((1 - odd) * rest, size)
    rest_start = pl.multiple_of((1 - odd) * width, size)

    def forward_edge(c):
        cut = pl.ds(outer_start, width)
        return pltpu.make_async_remote_copy(
            src_ref=zout.at[c, :, cut], dst_ref=zin.at[c, :, cut], send_sem=es.at[c], recv_sem=er.at[c],
            device_id={"section": after}, device_id_type=MESH)

    def forward(c):
        cut = pl.ds(rest_start, rest)
        return pltpu.make_async_remote_copy(
            src_ref=zout.at[c, :, cut], dst_ref=zin.at[c, :, cut], send_sem=zs.at[c], recv_sem=zr.at[c],
            device_id={"section": after}, device_id_type=MESH)

    def deliver(c):
        owner, slot, batch, row = place(c)
        target = out.at[batch, pl.ds(pl.multiple_of(row, rows), rows), :]
        return pltpu.make_async_remote_copy(
            src_ref=zout.at[c], dst_ref=target, send_sem=zs.at[c], recv_sem=og.at[slot],
            device_id={"section": owner}, device_id_type=MESH)

    def keep(c):
        _, _, batch, row = place(c)
        target = out.at[batch, pl.ds(pl.multiple_of(row, rows), rows), :]
        return pltpu.make_async_copy(zout.at[c], target, zs.at[c])

    def to_outer(c):
        return pltpu.make_async_remote_copy(
            src_ref=zin.at[c, :, pl.ds(outer_start, width)], dst_ref=ho.at[c], send_sem=os.at[c], recv_sem=orr.at[c],
            device_id={"neuron": outer}, device_id_type=MESH)

    def to_inner(c):
        return pltpu.make_async_remote_copy(
            src_ref=zin.at[c, :, pl.ds(inner_start, width)], dst_ref=hi.at[c], send_sem=ks.at[c], recv_sem=kr.at[c],
            device_id={"neuron": inner}, device_id_type=MESH)

    @pl.when(first)
    def _():
        for c in range(INNER):
            fetch(c).start()

    own_a = pltpu.make_async_copy(w.at[0], wa.at[pl.ds(HALO, blocks)], ws.at[0])
    own_b = pltpu.make_async_copy(w.at[1], wb, ws.at[1])
    own_a.start()
    own_b.start()

    @pl.when(first)
    def _():
        @pl.loop(INNER, chunks)
        def _(c):
            fetch(c).start()

    @pl.when(jnp.logical_or(first, last))
    def _():
        pl.semaphore_wait(barrier, 3)

    @pl.when(jnp.logical_not(jnp.logical_or(first, last)))
    def _():
        pl.semaphore_wait(barrier, 4)


    def receive_outer(c):
        @pl.when(jnp.logical_not(first))
        def _():
            forward_edge(c).wait_recv()

        to_outer(c).start()

    def receive_inner(c):
        @pl.when(first)
        def _():
            fetch(c).wait()

        @pl.when(jnp.logical_not(first))
        def _():
            forward(c).wait_recv()

        to_inner(c).start()

    def margin(k, source, target, device):
        return pltpu.make_async_remote_copy(
            src_ref=source, dst_ref=target, send_sem=ws.at[2 + k], recv_sem=wr.at[k],
            device_id={"neuron": device}, device_id_type=MESH)

    own_end = blocks - HALO
    outer_block, inner_block = odd * own_end, (1 - odd) * own_end
    edge_width = HALO * size

    def columns(block):
        return pl.ds(pl.multiple_of(block * size, size), edge_width)

    outer_margin = (1 - odd) * (HALO + blocks)
    inner_margin = odd * (HALO + blocks)
    inner_bias = margin(0, bias.at[:, columns(inner_block)], bi, inner)
    inner_weights = margin(1, w.at[0, pl.ds(inner_block, HALO)], wa.at[pl.ds(inner_margin, HALO)], inner)
    outer_bias = margin(2, bias.at[:, columns(outer_block)], bo, outer)
    outer_weights = margin(3, w.at[0, pl.ds(outer_block, HALO)], wa.at[pl.ds(outer_margin, HALO)], outer)

    @pl.when(first)
    def _():
        receive_inner(0)
        receive_outer(0)

    for copy in (inner_bias, inner_weights, outer_bias, outer_weights):
        copy.start()

    @pl.when(first)
    def _():
        for c in range(1, INNER):
            receive_inner(c)
            if c < OUTER:
                receive_outer(c)

    span = blocks + 2 * HALO

    def bias_rows(values, row, start, block):
        bs[start] = jnp.broadcast_to(values[row : row + 1, block * size : (block + 1) * size], (rows, size))

    own = bias[...].astype(jnp.float32)
    for j in range(blocks):
        bias_rows(own, 0, HALO + j, j)
        bias_rows(own, 1, span + j, j)
    inner_bias.wait()
    arrived = bi[...].astype(jnp.float32)
    for j in range(HALO):
        bias_rows(arrived, 0, (1 - odd) * (HALO + blocks) + j, j)
    own_a.wait()
    own_b.wait()
    inner_weights.wait()

    def apply(source, at, weights, pair, shift, bias_base):
        sums = [
            jnp.dot(
                jnp.concatenate([source[at + p + s] for s in shift[:2]], axis=1),
                weights[p, 0:2].reshape(2 * size, size),
                preferred_element_type=jnp.float32,
            )
            for p in pair
        ]
        zero = jnp.zeros((rows, size), jnp.bfloat16)
        third = jnp.concatenate(
            [
                jnp.concatenate([source[at + pair[0] + shift[2]], zero], axis=1),
                jnp.concatenate([zero, source[at + pair[1] + shift[2]]], axis=1),
            ],
            axis=0,
        )
        both = jnp.concatenate([weights[p, 2] for p in pair], axis=0)
        rest = jnp.dot(third, both, preferred_element_type=jnp.float32)
        done = []
        for k, p in enumerate(pair):
            total = sums[k] + rest[k * rows : (k + 1) * rows] + bs[bias_base + p]
            done.append(jnp.minimum(jnp.maximum(total, 0.0), ceiling).astype(jnp.bfloat16))
        return done

    reach = span + 2 * HALO

    def layer_a(slot, begin, end):
        for j in range(begin, end, 2):
            pair = [k + odd * (span - 1 - 2 * k) for k in (j, j + 1)]
            for p, block in zip(pair, apply(work, slot * reach, wa, pair, shift_a, 0)):
                mid[slot * span + p] = block

    def layer_b(c, slot, begin, end):
        for j in range(begin, end, 2):
            pair = [k + odd * (blocks - 1 - 2 * k) for k in (j, j + 1)]
            for p, block in zip(pair, apply(mid, slot * span, wb, pair, shift_b, span)):
                zout[c, :, pl.ds(pl.multiple_of(p * size, size), size)] = block

    def first_phase(c):
        slot = c % SLOTS
        for j in range(blocks):
            work[slot * reach + 2 * HALO + j] = zin[c, :, j * size : (j + 1) * size]
        to_inner(c).wait_recv()
        for j in range(2 * HALO):
            work[slot * reach + inner_base + j] = hi[c, :, j * size : (j + 1) * size]
        layer_a(slot, 2 * HALO, span)
        layer_b(c, slot, 2 * HALO, blocks)

        @pl.when(jnp.logical_not(last))
        def _():
            forward(c).start()

    def second_phase(c):
        slot = c % SLOTS
        to_outer(c).wait_recv()
        for j in range(2 * HALO):
            work[slot * reach + outer_base + j] = ho[c, :, j * size : (j + 1) * size]
        layer_a(slot, 0, 2 * HALO)
        layer_b(c, slot, 0, 2 * HALO)

    bands = w.shape[2]
    outer_base = odd * (2 * HALO + blocks)
    inner_base = (1 - odd) * (2 * HALO + blocks)
    shift_a = [offs[0, b] + HALO for b in range(bands)]
    shift_b = [offs[1, b] + HALO for b in range(bands)]

    later = jnp.logical_not(first)

    @pl.when(later)
    def _():
        for c in range(FIRST):
            receive_inner(c)
        receive_outer(0)

    first_phase(0)
    for c in range(1, FIRST):
        @pl.when(later)
        def _(c=c):
            if c == 1:
                receive_inner(FIRST)
            if c < OUTER:
                receive_outer(c)

        first_phase(c)

    @pl.when(later)
    def _():
        for c in range(max(FIRST, 1), OUTER):
            receive_outer(c)
        if FIRST == 1:
            receive_inner(FIRST)

    outer_bias.wait()
    arrived = bo[...].astype(jnp.float32)
    for j in range(HALO):
        bias_rows(arrived, 0, odd * (HALO + blocks) + j, j)
    outer_weights.wait()

    far = jnp.logical_or(me == 0, me == devices - 1)
    close = jnp.logical_not(far)

    @pl.loop(0, chunks)
    def _(c):
        @pl.when(jnp.logical_and(far, c + OUTER < chunks))
        def _():
            receive_outer(c + OUTER)

        second_phase(c)

        @pl.when(jnp.logical_not(last))
        def _():
            forward_edge(c).start()

        @pl.when(last)
        def _():
            @pl.when(c // per_owner < sections - 1)
            def _():
                deliver(c).start()

            @pl.when(c // per_owner == sections - 1)
            def _():
                keep(c).start()

        @pl.when(c + INNER < chunks)
        def _():
            receive_inner(c + INNER)

        @pl.when(jnp.logical_and(close, c + OUTER < chunks))
        def _():
            receive_outer(c + OUTER)

        @pl.when(c + FIRST < chunks)
        def _():
            first_phase(c + FIRST)

    @pl.loop(0, chunks)
    def _(c):
        to_outer(c).wait_send()
        to_inner(c).wait_send()

        @pl.when(jnp.logical_not(last))
        def _():
            forward_edge(c).wait_send()
            forward(c).wait_send()

        @pl.when(last)
        def _():
            @pl.when(c // per_owner < sections - 1)
            def _():
                deliver(c).wait_send()

            @pl.when(c // per_owner == sections - 1)
            def _():
                keep(c).wait()

    @pl.when(jnp.logical_not(last))
    def _():
        @pl.loop(0, per_owner)
        def _(c):
            deliver(c).wait_recv()


def shards(sections, devices, inputs, weights, bias, offsets):
    micro, row_count, local = inputs.shape
    layers, blocks, bands, size = weights.shape[:4]
    share = row_count // sections
    chunks = micro * row_count // ROWS
    span = blocks + 2 * HALO
    bf16, dma = jnp.bfloat16, pltpu.SemaphoreType.DMA
    dims = (sections, devices, micro, share, chunks, blocks, size)
    return pl.pallas_call(
        functools.partial(kernel, dims),
        out_shape=jax.ShapeDtypeStruct((micro, share, local), bf16),
        in_specs=[
            pl.BlockSpec(memory_space=pltpu.SMEM),
            pl.BlockSpec(memory_space=pl.ANY),
            pl.BlockSpec(memory_space=pl.ANY),
            pl.BlockSpec(memory_space=pltpu.VMEM),
        ],
        out_specs=pl.BlockSpec(memory_space=pl.ANY),
        scratch_shapes=[
            pltpu.VMEM((span, bands, size, size), bf16),
            pltpu.VMEM((blocks, bands, size, size), bf16),
            pltpu.VMEM((layers, HALO * size), bf16),
            pltpu.VMEM((layers, HALO * size), bf16),
            pltpu.VMEM((span + blocks, ROWS, size), jnp.float32),
            pltpu.VMEM((chunks, ROWS, local), bf16),
            pltpu.VMEM((chunks, ROWS, local), bf16),
            pltpu.VMEM((chunks, ROWS, 2 * HALO * size), bf16),
            pltpu.VMEM((chunks, ROWS, 2 * HALO * size), bf16),
            pltpu.VMEM((SLOTS * (span + 2 * HALO), ROWS, size), bf16),
            pltpu.VMEM((SLOTS * span, ROWS, size), bf16),
            *[dma((chunks,))] * 8,
            dma((micro * share // ROWS,)), dma((6,)), dma((4,)),
        ],
        compiler_params=pltpu.CompilerParams(collective_id=0, has_side_effects=True),
    )(offsets, inputs, weights, bias)


def solution(mesh):
    in_specs = (
        P(None, None, "neuron"),
        P("section", "neuron", None, None, None),
        P("section", "neuron"),
        P("section", None),
    )
    out_specs = P(None, "section", "neuron")
    body = functools.partial(shards, mesh.shape["section"], mesh.shape["neuron"])
    return jax.shard_map(body, mesh=mesh, in_specs=in_specs, out_specs=out_specs, check_vma=False)
```

```python
import functools

import jax
import jax.numpy as jnp
from jax import lax
from jax.experimental import pallas as pl
from jax.experimental.pallas import tpu as pltpu
from jax.sharding import PartitionSpec as P

MESH = pl.DeviceIdType.MESH
HALO = 3
ceiling = 2.0
ROWS = 16
OUTER = 3
REUSE = 8
FIRST = 3
INNER = FIRST + 1
SLOTS = FIRST + 1


def kernel(
    dims, offs, x, w, bias, out,
    wa, wb, bo, bi, bs, zin, zout, ho, hi, work, mid,
    es, er, zs, zr, os, orr, ks, kr, og, ws, wr,
):
    sections, devices, micro, share, chunks, blocks, size = dims
    rows = ROWS
    width = 2 * HALO * size
    sec = lax.axis_index("section")
    me = lax.axis_index("neuron")
    left = lax.rem(me + devices - 1, devices)
    right = lax.rem(me + 1, devices)
    after = lax.rem(sec + 1, sections)
    before = lax.rem(sec + sections - 1, sections)
    per_share = share // rows
    per_owner = micro * per_share

    barrier = pltpu.get_barrier_semaphore()
    first = sec == 0
    last = sec == sections - 1
    for where in ({"neuron": left}, {"neuron": right}):
        pl.semaphore_signal(barrier, inc=1, device_id=where, device_id_type=MESH)

    @pl.when(jnp.logical_not(last))
    def _():
        pl.semaphore_signal(barrier, inc=1, device_id={"section": after}, device_id_type=MESH)

    @pl.when(jnp.logical_not(first))
    def _():
        pl.semaphore_signal(barrier, inc=1, device_id={"section": before}, device_id_type=MESH)

    def place(c):
        owner = c // per_owner
        slot = c % per_owner
        batch = slot // per_share
        row = (slot % per_share) * rows
        return owner, slot, batch, row

    def fetch(c):
        owner, _, batch, row = place(c)
        start = pl.multiple_of(owner * share + row, rows)
        return pltpu.make_async_copy(x.at[batch, pl.ds(start, rows), :], zin.at[c], er.at[c])

    odd = lax.rem(me, 2)
    outer = lax.rem(me + devices - 1 + 2 * odd, devices)
    inner = me + 1 - 2 * odd
    rest = blocks * size - width
    outer_start = pl.multiple_of(odd * rest, size)
    inner_start = pl.multiple_of((1 - odd) * rest, size)
    rest_start = pl.multiple_of((1 - odd) * width, size)

    def forward_edge(c):
        cut = pl.ds(outer_start, width)
        return pltpu.make_async_remote_copy(
            src_ref=zout.at[c, :, cut], dst_ref=zin.at[c, :, cut], send_sem=es.at[c % REUSE], recv_sem=er.at[c],
            device_id={"section": after}, device_id_type=MESH)

    def forward(c):
        cut = pl.ds(rest_start, rest)
        return pltpu.make_async_remote_copy(
            src_ref=zout.at[c, :, cut], dst_ref=zin.at[c, :, cut], send_sem=zs.at[c % REUSE], recv_sem=zr.at[c],
            device_id={"section": after}, device_id_type=MESH)

    def deliver(c):
        owner, slot, batch, row = place(c)
        target = out.at[batch, pl.ds(pl.multiple_of(row, rows), rows), :]
        return pltpu.make_async_remote_copy(
            src_ref=zout.at[c], dst_ref=target, send_sem=zs.at[c % REUSE], recv_sem=og.at[slot],
            device_id={"section": owner}, device_id_type=MESH)

    def keep(c):
        _, _, batch, row = place(c)
        target = out.at[batch, pl.ds(pl.multiple_of(row, rows), rows), :]
        return pltpu.make_async_copy(zout.at[c], target, zs.at[c % REUSE])

    def to_outer(c):
        return pltpu.make_async_remote_copy(
            src_ref=zin.at[c, :, pl.ds(outer_start, width)], dst_ref=ho.at[c], send_sem=os.at[c % REUSE], recv_sem=orr.at[c],
            device_id={"neuron": outer}, device_id_type=MESH)

    def to_inner(c):
        return pltpu.make_async_remote_copy(
            src_ref=zin.at[c, :, pl.ds(inner_start, width)], dst_ref=hi.at[c], send_sem=ks.at[c % REUSE], recv_sem=kr.at[c],
            device_id={"neuron": inner}, device_id_type=MESH)

    @pl.when(first)
    def _():
        for c in range(INNER):
            fetch(c).start()

    own_a = pltpu.make_async_copy(w.at[0], wa.at[pl.ds(HALO, blocks)], ws.at[0])
    own_b = pltpu.make_async_copy(w.at[1], wb, ws.at[1])
    own_a.start()
    own_b.start()

    @pl.when(first)
    def _():
        @pl.loop(INNER, chunks)
        def _(c):
            fetch(c).start()

    @pl.when(jnp.logical_or(first, last))
    def _():
        pl.semaphore_wait(barrier, 3)

    @pl.when(jnp.logical_not(jnp.logical_or(first, last)))
    def _():
        pl.semaphore_wait(barrier, 4)


    def receive_outer(c):
        @pl.when(jnp.logical_not(first))
        def _():
            forward_edge(c).wait_recv()

        if not isinstance(c, int):
            @pl.when(c >= REUSE)
            def _():
                to_outer(c - REUSE).wait_send()

        to_outer(c).start()

    def receive_inner(c):
        @pl.when(first)
        def _():
            fetch(c).wait()

        @pl.when(jnp.logical_not(first))
        def _():
            forward(c).wait_recv()

        if not isinstance(c, int):
            @pl.when(c >= REUSE)
            def _():
                to_inner(c - REUSE).wait_send()

        to_inner(c).start()

    def margin(k, source, target, device):
        return pltpu.make_async_remote_copy(
            src_ref=source, dst_ref=target, send_sem=ws.at[2 + k], recv_sem=wr.at[k],
            device_id={"neuron": device}, device_id_type=MESH)

    own_end = blocks - HALO
    outer_block, inner_block = odd * own_end, (1 - odd) * own_end
    edge_width = HALO * size

    def columns(block):
        return pl.ds(pl.multiple_of(block * size, size), edge_width)

    outer_margin = (1 - odd) * (HALO + blocks)
    inner_margin = odd * (HALO + blocks)
    inner_bias = margin(0, bias.at[:, columns(inner_block)], bi, inner)
    inner_weights = margin(1, w.at[0, pl.ds(inner_block, HALO)], wa.at[pl.ds(inner_margin, HALO)], inner)
    outer_bias = margin(2, bias.at[:, columns(outer_block)], bo, outer)
    outer_weights = margin(3, w.at[0, pl.ds(outer_block, HALO)], wa.at[pl.ds(outer_margin, HALO)], outer)

    @pl.when(first)
    def _():
        receive_inner(0)
        receive_outer(0)

    for copy in (inner_bias, inner_weights, outer_bias, outer_weights):
        copy.start()

    @pl.when(first)
    def _():
        for c in range(1, INNER):
            receive_inner(c)
            if c < OUTER:
                receive_outer(c)

    span = blocks + 2 * HALO

    def bias_rows(values, row, start, block):
        bs[start] = jnp.broadcast_to(values[row : row + 1, block * size : (block + 1) * size], (rows, size))

    own = bias[...].astype(jnp.float32)
    for j in range(blocks):
        bias_rows(own, 0, HALO + j, j)
        bias_rows(own, 1, span + j, j)
    inner_bias.wait()
    arrived = bi[...].astype(jnp.float32)
    for j in range(HALO):
        bias_rows(arrived, 0, (1 - odd) * (HALO + blocks) + j, j)
    own_a.wait()
    own_b.wait()
    inner_weights.wait()

    def apply(source, at, weights, pair, shift, bias_base):
        sums = [
            jnp.dot(
                jnp.concatenate([source[at + p + s] for s in shift[:2]], axis=1),
                weights[p, 0:2].reshape(2 * size, size),
                preferred_element_type=jnp.float32,
            )
            for p in pair
        ]
        zero = jnp.zeros((rows, size), jnp.bfloat16)
        third = jnp.concatenate(
            [
                jnp.concatenate([source[at + pair[0] + shift[2]], zero], axis=1),
                jnp.concatenate([zero, source[at + pair[1] + shift[2]]], axis=1),
            ],
            axis=0,
        )
        both = jnp.concatenate([weights[p, 2] for p in pair], axis=0)
        rest = jnp.dot(third, both, preferred_element_type=jnp.float32)
        done = []
        for k, p in enumerate(pair):
            total = sums[k] + rest[k * rows : (k + 1) * rows] + bs[bias_base + p]
            done.append(jnp.minimum(jnp.maximum(total, 0.0), ceiling).astype(jnp.bfloat16))
        return done

    reach = span + 2 * HALO

    def layer_a(slot, begin, end):
        for j in range(begin, end, 2):
            pair = [k + odd * (span - 1 - 2 * k) for k in (j, j + 1)]
            for p, block in zip(pair, apply(work, slot * reach, wa, pair, shift_a, 0)):
                mid[slot * span + p] = block

    def layer_b(c, slot, begin, end):
        for j in range(begin, end, 2):
            pair = [k + odd * (blocks - 1 - 2 * k) for k in (j, j + 1)]
            for p, block in zip(pair, apply(mid, slot * span, wb, pair, shift_b, span)):
                zout[c, :, pl.ds(pl.multiple_of(p * size, size), size)] = block

    def first_phase(c):
        slot = c % SLOTS
        for j in range(blocks):
            work[slot * reach + 2 * HALO + j] = zin[c, :, j * size : (j + 1) * size]
        to_inner(c).wait_recv()
        for j in range(2 * HALO):
            work[slot * reach + inner_base + j] = hi[c, :, j * size : (j + 1) * size]
        layer_a(slot, 2 * HALO, span)
        layer_b(c, slot, 2 * HALO, blocks)

        @pl.when(jnp.logical_not(last))
        def _():
            if not isinstance(c, int):
                @pl.when(c >= REUSE)
                def _():
                    forward(c - REUSE).wait_send()

            forward(c).start()

    def second_phase(c):
        slot = c % SLOTS
        to_outer(c).wait_recv()
        for j in range(2 * HALO):
            work[slot * reach + outer_base + j] = ho[c, :, j * size : (j + 1) * size]
        layer_a(slot, 0, 2 * HALO)
        layer_b(c, slot, 0, 2 * HALO)

    bands = w.shape[2]
    outer_base = odd * (2 * HALO + blocks)
    inner_base = (1 - odd) * (2 * HALO + blocks)
    shift_a = [offs[0, b] + HALO for b in range(bands)]
    shift_b = [offs[1, b] + HALO for b in range(bands)]

    later = jnp.logical_not(first)

    @pl.when(later)
    def _():
        for c in range(FIRST):
            receive_inner(c)
        receive_outer(0)

    first_phase(0)
    for c in range(1, FIRST):
        @pl.when(later)
        def _(c=c):
            if c == 1:
                receive_inner(FIRST)
            if c < OUTER:
                receive_outer(c)

        first_phase(c)

    @pl.when(later)
    def _():
        for c in range(max(FIRST, 1), OUTER):
            receive_outer(c)
        if FIRST == 1:
            receive_inner(FIRST)

    outer_bias.wait()
    arrived = bo[...].astype(jnp.float32)
    for j in range(HALO):
        bias_rows(arrived, 0, odd * (HALO + blocks) + j, j)
    outer_weights.wait()

    far = jnp.logical_or(me == 0, me == devices - 1)
    close = jnp.logical_not(far)

    @pl.loop(0, chunks)
    def _(c):
        @pl.when(jnp.logical_and(far, c + OUTER < chunks))
        def _():
            receive_outer(c + OUTER)

        second_phase(c)

        @pl.when(jnp.logical_not(last))
        def _():
            @pl.when(c >= REUSE)
            def _():
                forward_edge(c - REUSE).wait_send()

            forward_edge(c).start()

        @pl.when(last)
        def _():
            @pl.when(c // per_owner < sections - 1)
            def _():
                @pl.when(c >= REUSE)
                def _():
                    deliver(c - REUSE).wait_send()

                deliver(c).start()

            @pl.when(c // per_owner == sections - 1)
            def _():
                deliver(c - REUSE).wait_send()
                keep(c).start()

        @pl.when(c + INNER < chunks)
        def _():
            receive_inner(c + INNER)

        @pl.when(jnp.logical_and(close, c + OUTER < chunks))
        def _():
            receive_outer(c + OUTER)

        @pl.when(c + FIRST < chunks)
        def _():
            first_phase(c + FIRST)

    @pl.loop(chunks - REUSE, chunks)
    def _(c):
        to_outer(c).wait_send()
        to_inner(c).wait_send()

        @pl.when(jnp.logical_not(last))
        def _():
            forward_edge(c).wait_send()
            forward(c).wait_send()

        @pl.when(last)
        def _():
            @pl.when(c // per_owner < sections - 1)
            def _():
                deliver(c).wait_send()

            @pl.when(c // per_owner == sections - 1)
            def _():
                keep(c).wait()

    @pl.when(jnp.logical_not(last))
    def _():
        @pl.loop(0, per_owner)
        def _(c):
            deliver(c).wait_recv()


def shards(sections, devices, inputs, weights, bias, offsets):
    micro, row_count, local = inputs.shape
    layers, blocks, bands, size = weights.shape[:4]
    share = row_count // sections
    chunks = micro * row_count // ROWS
    span = blocks + 2 * HALO
    bf16, dma = jnp.bfloat16, pltpu.SemaphoreType.DMA
    dims = (sections, devices, micro, share, chunks, blocks, size)
    return pl.pallas_call(
        functools.partial(kernel, dims),
        out_shape=jax.ShapeDtypeStruct((micro, share, local), bf16),
        in_specs=[
            pl.BlockSpec(memory_space=pltpu.SMEM),
            pl.BlockSpec(memory_space=pl.ANY),
            pl.BlockSpec(memory_space=pl.ANY),
            pl.BlockSpec(memory_space=pltpu.VMEM),
        ],
        out_specs=pl.BlockSpec(memory_space=pl.ANY),
        scratch_shapes=[
            pltpu.VMEM((span, bands, size, size), bf16),
            pltpu.VMEM((blocks, bands, size, size), bf16),
            pltpu.VMEM((layers, HALO * size), bf16),
            pltpu.VMEM((layers, HALO * size), bf16),
            pltpu.VMEM((span + blocks, ROWS, size), jnp.float32),
            pltpu.VMEM((chunks, ROWS, local), bf16),
            pltpu.VMEM((chunks, ROWS, local), bf16),
            pltpu.VMEM((chunks, ROWS, 2 * HALO * size), bf16),
            pltpu.VMEM((chunks, ROWS, 2 * HALO * size), bf16),
            pltpu.VMEM((SLOTS * (span + 2 * HALO), ROWS, size), bf16),
            pltpu.VMEM((SLOTS * span, ROWS, size), bf16),
            *[dma((REUSE,)), dma((chunks,))] * 2, *[dma((REUSE,)), dma((chunks,))] * 2,
            dma((micro * share // ROWS,)), dma((6,)), dma((4,)),
        ],
        compiler_params=pltpu.CompilerParams(collective_id=0, has_side_effects=True),
    )(offsets, inputs, weights, bias)


def solution(mesh):
    in_specs = (
        P(None, None, "neuron"),
        P("section", "neuron", None, None, None),
        P("section", "neuron"),
        P("section", None),
    )
    out_specs = P(None, "section", "neuron")
    body = functools.partial(shards, mesh.shape["section"], mesh.shape["neuron"])
    return jax.shard_map(body, mesh=mesh, in_specs=in_specs, out_specs=out_specs, check_vma=False)
```

```python
import functools

import jax
import jax.numpy as jnp
from jax import lax
from jax.experimental import pallas as pl
from jax.experimental.pallas import tpu as pltpu
from jax.sharding import PartitionSpec as P

MESH = pl.DeviceIdType.MESH
HALO = 3
ceiling = 2.0
ROWS = 16
OUTER = 3
REUSE = 8
FIRST = 3
INNER = FIRST + 1
SLOTS = FIRST + 1


def kernel(
    dims, offs, x, w, bias, out,
    wa, wb, bo, bi, bs, zin, zout, ho, hi, work, mid,
    es, er, zs, zr, os, orr, ks, kr, og, ws, wr,
):
    sections, devices, micro, share, chunks, blocks, size = dims
    rows = ROWS
    width = 2 * HALO * size
    sec = lax.axis_index("section")
    me = lax.axis_index("neuron")
    left = lax.rem(me + devices - 1, devices)
    right = lax.rem(me + 1, devices)
    after = lax.rem(sec + 1, sections)
    before = lax.rem(sec + sections - 1, sections)
    per_share = share // rows
    per_owner = micro * per_share

    barrier = pltpu.get_barrier_semaphore()
    first = sec == 0
    last = sec == sections - 1
    for where in ({"neuron": left}, {"neuron": right}):
        pl.semaphore_signal(barrier, inc=1, device_id=where, device_id_type=MESH)

    @pl.when(jnp.logical_not(last))
    def _():
        pl.semaphore_signal(barrier, inc=1, device_id={"section": after}, device_id_type=MESH)

    @pl.when(jnp.logical_not(first))
    def _():
        pl.semaphore_signal(barrier, inc=1, device_id={"section": before}, device_id_type=MESH)

    def place(c):
        owner = c // per_owner
        slot = c % per_owner
        batch = slot // per_share
        row = (slot % per_share) * rows
        return owner, slot, batch, row

    def fetch(c):
        owner, _, batch, row = place(c)
        start = pl.multiple_of(owner * share + row, rows)
        return pltpu.make_async_copy(x.at[batch, pl.ds(start, rows), :], zin.at[c], er.at[c])

    odd = lax.rem(me, 2)
    outer = lax.rem(me + devices - 1 + 2 * odd, devices)
    inner = me + 1 - 2 * odd
    rest = blocks * size - width
    outer_start = pl.multiple_of(odd * rest, size)
    inner_start = pl.multiple_of((1 - odd) * rest, size)
    rest_start = pl.multiple_of((1 - odd) * width, size)

    def forward_edge(c):
        cut = pl.ds(outer_start, width)
        return pltpu.make_async_remote_copy(
            src_ref=zout.at[c, :, cut], dst_ref=zin.at[c, :, cut], send_sem=es.at[c % REUSE], recv_sem=er.at[c],
            device_id={"section": after}, device_id_type=MESH)

    def forward(c):
        cut = pl.ds(rest_start, rest)
        return pltpu.make_async_remote_copy(
            src_ref=zout.at[c, :, cut], dst_ref=zin.at[c, :, cut], send_sem=zs.at[c % REUSE], recv_sem=zr.at[c],
            device_id={"section": after}, device_id_type=MESH)

    def deliver(c):
        owner, slot, batch, row = place(c)
        target = out.at[batch, pl.ds(pl.multiple_of(row, rows), rows), :]
        return pltpu.make_async_remote_copy(
            src_ref=zout.at[c], dst_ref=target, send_sem=zs.at[c % REUSE], recv_sem=og.at[slot],
            device_id={"section": owner}, device_id_type=MESH)

    def keep(c):
        _, _, batch, row = place(c)
        target = out.at[batch, pl.ds(pl.multiple_of(row, rows), rows), :]
        return pltpu.make_async_copy(zout.at[c], target, zs.at[c % REUSE])

    def to_outer(c):
        return pltpu.make_async_remote_copy(
            src_ref=zin.at[c, :, pl.ds(outer_start, width)], dst_ref=ho.at[c], send_sem=os.at[c % REUSE], recv_sem=orr.at[c % REUSE],
            device_id={"neuron": outer}, device_id_type=MESH)

    def to_inner(c):
        return pltpu.make_async_remote_copy(
            src_ref=zin.at[c, :, pl.ds(inner_start, width)], dst_ref=hi.at[c], send_sem=ks.at[c % REUSE], recv_sem=kr.at[c % REUSE],
            device_id={"neuron": inner}, device_id_type=MESH)

    @pl.when(first)
    def _():
        for c in range(INNER):
            fetch(c).start()

    own_a = pltpu.make_async_copy(w.at[0], wa.at[pl.ds(HALO, blocks)], ws.at[0])
    own_b = pltpu.make_async_copy(w.at[1], wb, ws.at[1])
    own_a.start()
    own_b.start()

    @pl.when(first)
    def _():
        @pl.loop(INNER, chunks)
        def _(c):
            fetch(c).start()

    @pl.when(jnp.logical_or(first, last))
    def _():
        pl.semaphore_wait(barrier, 3)

    @pl.when(jnp.logical_not(jnp.logical_or(first, last)))
    def _():
        pl.semaphore_wait(barrier, 4)


    def receive_outer(c):
        @pl.when(jnp.logical_not(first))
        def _():
            forward_edge(c).wait_recv()

        if not isinstance(c, int):
            @pl.when(c >= REUSE)
            def _():
                to_outer(c - REUSE).wait_send()

        to_outer(c).start()

    def receive_inner(c):
        @pl.when(first)
        def _():
            fetch(c).wait()

        @pl.when(jnp.logical_not(first))
        def _():
            forward(c).wait_recv()

        if not isinstance(c, int):
            @pl.when(c >= REUSE)
            def _():
                to_inner(c - REUSE).wait_send()

        to_inner(c).start()

    def margin(k, source, target, device):
        return pltpu.make_async_remote_copy(
            src_ref=source, dst_ref=target, send_sem=ws.at[2 + k], recv_sem=wr.at[k],
            device_id={"neuron": device}, device_id_type=MESH)

    own_end = blocks - HALO
    outer_block, inner_block = odd * own_end, (1 - odd) * own_end
    edge_width = HALO * size

    def columns(block):
        return pl.ds(pl.multiple_of(block * size, size), edge_width)

    outer_margin = (1 - odd) * (HALO + blocks)
    inner_margin = odd * (HALO + blocks)
    inner_bias = margin(0, bias.at[:, columns(inner_block)], bi, inner)
    inner_weights = margin(1, w.at[0, pl.ds(inner_block, HALO)], wa.at[pl.ds(inner_margin, HALO)], inner)
    outer_bias = margin(2, bias.at[:, columns(outer_block)], bo, outer)
    outer_weights = margin(3, w.at[0, pl.ds(outer_block, HALO)], wa.at[pl.ds(outer_margin, HALO)], outer)

    @pl.when(first)
    def _():
        receive_inner(0)
        receive_outer(0)

    for copy in (inner_bias, inner_weights, outer_bias, outer_weights):
        copy.start()

    @pl.when(first)
    def _():
        for c in range(1, INNER):
            receive_inner(c)
            if c < OUTER:
                receive_outer(c)

    span = blocks + 2 * HALO

    def bias_rows(values, row, start, block):
        bs[start] = jnp.broadcast_to(values[row : row + 1, block * size : (block + 1) * size], (rows, size))

    own = bias[...].astype(jnp.float32)
    for j in range(blocks):
        bias_rows(own, 0, HALO + j, j)
        bias_rows(own, 1, span + j, j)
    inner_bias.wait()
    arrived = bi[...].astype(jnp.float32)
    for j in range(HALO):
        bias_rows(arrived, 0, (1 - odd) * (HALO + blocks) + j, j)
    own_a.wait()
    own_b.wait()
    inner_weights.wait()

    def apply(source, at, weights, pair, shift, bias_base):
        sums = [
            jnp.dot(
                jnp.concatenate([source[at + p + s] for s in shift[:2]], axis=1),
                weights[p, 0:2].reshape(2 * size, size),
                preferred_element_type=jnp.float32,
            )
            for p in pair
        ]
        zero = jnp.zeros((rows, size), jnp.bfloat16)
        third = jnp.concatenate(
            [
                jnp.concatenate([source[at + pair[0] + shift[2]], zero], axis=1),
                jnp.concatenate([zero, source[at + pair[1] + shift[2]]], axis=1),
            ],
            axis=0,
        )
        both = jnp.concatenate([weights[p, 2] for p in pair], axis=0)
        rest = jnp.dot(third, both, preferred_element_type=jnp.float32)
        done = []
        for k, p in enumerate(pair):
            total = sums[k] + rest[k * rows : (k + 1) * rows] + bs[bias_base + p]
            done.append(jnp.minimum(jnp.maximum(total, 0.0), ceiling).astype(jnp.bfloat16))
        return done

    reach = span + 2 * HALO

    def layer_a(slot, begin, end):
        for j in range(begin, end, 2):
            pair = [k + odd * (span - 1 - 2 * k) for k in (j, j + 1)]
            for p, block in zip(pair, apply(work, slot * reach, wa, pair, shift_a, 0)):
                mid[slot * span + p] = block

    def layer_b(c, slot, begin, end):
        for j in range(begin, end, 2):
            pair = [k + odd * (blocks - 1 - 2 * k) for k in (j, j + 1)]
            for p, block in zip(pair, apply(mid, slot * span, wb, pair, shift_b, span)):
                zout[c, :, pl.ds(pl.multiple_of(p * size, size), size)] = block

    def first_phase(c):
        slot = c % SLOTS
        for j in range(blocks):
            work[slot * reach + 2 * HALO + j] = zin[c, :, j * size : (j + 1) * size]
        to_inner(c).wait_recv()
        for j in range(2 * HALO):
            work[slot * reach + inner_base + j] = hi[c, :, j * size : (j + 1) * size]
        layer_a(slot, 2 * HALO, span)
        layer_b(c, slot, 2 * HALO, blocks)

        @pl.when(jnp.logical_not(last))
        def _():
            if not isinstance(c, int):
                @pl.when(c >= REUSE)
                def _():
                    forward(c - REUSE).wait_send()

            forward(c).start()

    def second_phase(c):
        slot = c % SLOTS
        to_outer(c).wait_recv()
        for j in range(2 * HALO):
            work[slot * reach + outer_base + j] = ho[c, :, j * size : (j + 1) * size]
        layer_a(slot, 0, 2 * HALO)
        layer_b(c, slot, 0, 2 * HALO)

    bands = w.shape[2]
    outer_base = odd * (2 * HALO + blocks)
    inner_base = (1 - odd) * (2 * HALO + blocks)
    shift_a = [offs[0, b] + HALO for b in range(bands)]
    shift_b = [offs[1, b] + HALO for b in range(bands)]

    later = jnp.logical_not(first)

    @pl.when(later)
    def _():
        for c in range(FIRST):
            receive_inner(c)
        receive_outer(0)

    first_phase(0)
    for c in range(1, FIRST):
        @pl.when(later)
        def _(c=c):
            if c == 1:
                receive_inner(FIRST)
            if c < OUTER:
                receive_outer(c)

        first_phase(c)

    @pl.when(later)
    def _():
        for c in range(max(FIRST, 1), OUTER):
            receive_outer(c)
        if FIRST == 1:
            receive_inner(FIRST)

    outer_bias.wait()
    arrived = bo[...].astype(jnp.float32)
    for j in range(HALO):
        bias_rows(arrived, 0, odd * (HALO + blocks) + j, j)
    outer_weights.wait()

    far = jnp.logical_or(me == 0, me == devices - 1)
    close = jnp.logical_not(far)

    @pl.loop(0, chunks)
    def _(c):
        @pl.when(jnp.logical_and(far, c + OUTER < chunks))
        def _():
            receive_outer(c + OUTER)

        second_phase(c)

        @pl.when(jnp.logical_not(last))
        def _():
            @pl.when(c >= REUSE)
            def _():
                forward_edge(c - REUSE).wait_send()

            forward_edge(c).start()

        @pl.when(last)
        def _():
            @pl.when(c // per_owner < sections - 1)
            def _():
                @pl.when(c >= REUSE)
                def _():
                    deliver(c - REUSE).wait_send()

                deliver(c).start()

            @pl.when(c // per_owner == sections - 1)
            def _():
                deliver(c - REUSE).wait_send()
                keep(c).start()

        @pl.when(c + INNER < chunks)
        def _():
            receive_inner(c + INNER)

        @pl.when(jnp.logical_and(close, c + OUTER < chunks))
        def _():
            receive_outer(c + OUTER)

        @pl.when(c + FIRST < chunks)
        def _():
            first_phase(c + FIRST)

    @pl.loop(chunks - REUSE, chunks)
    def _(c):
        to_outer(c).wait_send()
        to_inner(c).wait_send()

        @pl.when(jnp.logical_not(last))
        def _():
            forward_edge(c).wait_send()
            forward(c).wait_send()

        @pl.when(last)
        def _():
            @pl.when(c // per_owner < sections - 1)
            def _():
                deliver(c).wait_send()

            @pl.when(c // per_owner == sections - 1)
            def _():
                keep(c).wait()

    @pl.when(jnp.logical_not(last))
    def _():
        @pl.loop(0, per_owner)
        def _(c):
            deliver(c).wait_recv()


def shards(sections, devices, inputs, weights, bias, offsets):
    micro, row_count, local = inputs.shape
    layers, blocks, bands, size = weights.shape[:4]
    share = row_count // sections
    chunks = micro * row_count // ROWS
    span = blocks + 2 * HALO
    bf16, dma = jnp.bfloat16, pltpu.SemaphoreType.DMA
    dims = (sections, devices, micro, share, chunks, blocks, size)
    return pl.pallas_call(
        functools.partial(kernel, dims),
        out_shape=jax.ShapeDtypeStruct((micro, share, local), bf16),
        in_specs=[
            pl.BlockSpec(memory_space=pltpu.SMEM),
            pl.BlockSpec(memory_space=pl.ANY),
            pl.BlockSpec(memory_space=pl.ANY),
            pl.BlockSpec(memory_space=pltpu.VMEM),
        ],
        out_specs=pl.BlockSpec(memory_space=pl.ANY),
        scratch_shapes=[
            pltpu.VMEM((span, bands, size, size), bf16),
            pltpu.VMEM((blocks, bands, size, size), bf16),
            pltpu.VMEM((layers, HALO * size), bf16),
            pltpu.VMEM((layers, HALO * size), bf16),
            pltpu.VMEM((span + blocks, ROWS, size), jnp.float32),
            pltpu.VMEM((chunks, ROWS, local), bf16),
            pltpu.VMEM((chunks, ROWS, local), bf16),
            pltpu.VMEM((chunks, ROWS, 2 * HALO * size), bf16),
            pltpu.VMEM((chunks, ROWS, 2 * HALO * size), bf16),
            pltpu.VMEM((SLOTS * (span + 2 * HALO), ROWS, size), bf16),
            pltpu.VMEM((SLOTS * span, ROWS, size), bf16),
            *[dma((REUSE,)), dma((chunks,))] * 2, *[dma((REUSE,))] * 4,
            dma((micro * share // ROWS,)), dma((6,)), dma((4,)),
        ],
        compiler_params=pltpu.CompilerParams(collective_id=0, has_side_effects=True),
    )(offsets, inputs, weights, bias)


def solution(mesh):
    in_specs = (
        P(None, None, "neuron"),
        P("section", "neuron", None, None, None),
        P("section", "neuron"),
        P("section", None),
    )
    out_specs = P(None, "section", "neuron")
    body = functools.partial(shards, mesh.shape["section"], mesh.shape["neuron"])
    return jax.shard_map(body, mesh=mesh, in_specs=in_specs, out_specs=out_specs, check_vma=False)
```
